32 devices in a mesh: dp: 16 (over z, y, x), tensor: 2 (over core).
Axes of the slice: x: 2, y: 2, z: 4, core: 2. Of those that a mesh axis runs over, the one named last changes fastest.
Arguments:
- tokens: bfloat16 [16, 1024, 768], P('dp'), may hold values from -6 to 6
- cotangent: bfloat16 [16, 1024, 768], P('dp'), may hold values from -6 to 6
- image_ids: int32 [16, 1024], P('dp'), may hold values from 0 to 3, never falling along the last dimension, each value on 1 to 512 neighbouring positions
- step_rates: float32 [2], replicated, may hold values from 0.2 to 0.6
- w_qkv: float32 [768, 3, 768], P('dp', None, 'tensor'), may hold values from -0.21875 to 0.21875
- w_out: float32 [768, 768], P('tensor', 'dp'), may hold values from -1.75 to 1.75
- w_up: float32 [768, 3072], P('dp', 'tensor'), may hold values from -0.4375 to 0.4375
- w_down: float32 [3072, 768], P('tensor', 'dp'), may hold values from -0.21875 to 0.21875
- norm_gains: float32 [2, 768], replicated, may hold values from 0.5 to 1.5
- row_biases: float32 [4, 768], replicated, may hold values from -1.8 to 1.8
- head_gains: float32 [2, 64], replicated, may hold values from 0.5 to 1.5
- query_bias: float32 [64], replicated, may hold values from -1.8 to 1.8
- qkv_bias: float32 [3, 768], P(None, 'tensor'), may hold values from -1.8 to 1.8
- hidden_bias: float32 [3072], P('tensor'), may hold values from -1.8 to 1.8
- mom_qkv: float32 [768, 3, 768], P('dp', None, 'tensor'), may hold values from -384 to 384
- mom_out: float32 [768, 768], P('tensor', 'dp'), may hold values from -384 to 14572.96
- mom_up: float32 [768, 3072], P('dp', 'tensor'), may hold values from -384 to 384
- mom_down: float32 [3072, 768], P('tensor', 'dp'), may hold values from -384 to 384
- mom_gains: float32 [2, 768], replicated, may hold values from -1024 to 1024
- mom_biases: float32 [4, 768], replicated, may hold values from -1536 to 1536
- mom_head_gains: float32 [2, 64], replicated, may hold values from -2048 to 2048
- mom_query_bias: float32 [64], replicated, may hold values from -3072 to 3072
- mom_qkv_bias: float32 [3, 768], P(None, 'tensor'), may hold values from -1536 to 1536
- mom_hidden_bias: float32 [3072], P('tensor'), may hold values from -384 to 384
Outputs:
- block_out: float32 [16, 1024, 768], P('dp')
- tokens_grad: float32 [16, 1024, 768], P('dp')
- grad_qkv: float32 [768, 3, 768], P('dp', None, 'tensor')
- grad_out: float32 [768, 768], P('tensor', 'dp')
- grad_up: float32 [768, 3072], P('dp', 'tensor')
- grad_down: float32 [3072, 768], P('tensor', 'dp')
- grad_gains: float32 [2, 768], replicated
- grad_biases: float32 [4, 768], replicated
- grad_head_gains: float32 [2, 64], replicated
- grad_query_bias: float32 [64], replicated
- grad_qkv_bias: float32 [3, 768], P(None, 'tensor')
- grad_hidden_bias: float32 [3072], P('tensor')
- next_mom_qkv: float32 [768, 3, 768], P('dp', None, 'tensor')
- next_mom_out: float32 [768, 768], P('tensor', 'dp')
- next_mom_up: float32 [768, 3072], P('dp', 'tensor')
- next_mom_down: float32 [3072, 768], P('tensor', 'dp')
- next_mom_gains: float32 [2, 768], replicated
- next_mom_biases: float32 [4, 768], replicated
- next_mom_head_gains: float32 [2, 64], replicated
- next_mom_query_bias: float32 [64], replicated
- next_mom_qkv_bias: float32 [3, 768], P(None, 'tensor')
- next_mom_hidden_bias: float32 [3072], P('tensor')
- new_w_qkv: float32 [768, 3, 768], P('dp', None, 'tensor')
- new_w_out: float32 [768, 768], P('tensor', 'dp')
- new_w_up: float32 [768, 3072], P('dp', 'tensor')
- new_w_down: float32 [3072, 768], P('tensor', 'dp')
- new_gains: float32 [2, 768], replicated
- new_biases: float32 [4, 768], replicated
- new_head_gains: float32 [2, 64], replicated
- new_query_bias: float32 [64], replicated
- new_qkv_bias: float32 [3, 768], P(None, 'tensor')
- new_hidden_bias: float32 [3072], P('tensor')
The draws below stay inside these ranges and needn't reach their ends.
Inputs may be any that keep to these rules, and one draw needn't show every extreme that they name: `image_ids`: within each row of 1024 patches the ids never fall; each of the 4 images has 1 to 512 patches.
All inputs are finite; a program needn't handle non-finite values.
Results may differ from the reference program's by a relative error of at most 0.025.
Values may be sent and summed in bfloat16 or wider, within the bound.
No kernel may reach another device: no remote copies, remote signals or barrier semaphores. Data moves between devices by JAX's collectives and lax.ppermute only.
A program may use at most 256 MiB of HBM per device.

```python
import math
import jax
import jax.numpy as jnp
import numpy as np
from jax import lax

D = 768
DH = 64
FF = 3072
LEN = 1024
IMG_SEQ = 4
IMG_MOST = 512
NS_ITERS = 5
SEQS = 16
TOKENS = 16384
N_TENSOR = 2


def draw_mom_out(key, part):
    base_key = jax.random.fold_in(key, 31)
    noise = jnp.clip(jax.random.normal(base_key, (D, D), jnp.float32), -6.0, 6.0)
    rows = jnp.arange(D)
    diagonal = (rows[:, None] == rows[None, :]).astype(jnp.float32)
    scale = 0.5 * jnp.sqrt(jnp.float32(TOKENS))
    return scale * (noise + 8.0 * jnp.sqrt(jnp.float32(D)) * diagonal)


def steps_of(rng, shape, shards, least, top_value):
    def one(axis_at, blocks):
        draws = jax.random.uniform(jax.random.fold_in(jax.random.fold_in(rng, 6), axis_at), (blocks,), jnp.float32, least / len(shards), top_value / len(shards))
        return jnp.repeat(jnp.exp(draws), shape[axis_at] // blocks).reshape((-1,) + (1,) * (len(shape) - axis_at - 1))

    gain = one(*shards[0])
    for cut in shards[1:]:
        gain = gain * one(*cut)
    return gain


def length_profile(count, total, reach, lean):
    weights = [(1 << 20) // math.isqrt(grade ** lean) + 1 for grade in range(2, count + 1)]
    rest, holding = total - reach - (count - 1), [1] * (count - 1)
    while rest > 0:
        candidates = [i for i in range(count - 1) if holding[i] < reach]
        pool, budget = sum([weights[i] for i in candidates]), rest
        for i in candidates:
            more = min(reach - holding[i], max(1, budget * weights[i] // pool), rest)
            holding[i] = holding[i] + more
            rest = rest - more
    return np.array([reach] + holding)


def ragged(stream_key, number_of, total, bound, skew):
    if number_of == 2:
        one = jax.random.randint(stream_key, (), max(1, total - bound), min(bound, total - 1) + 1)
        return jnp.stack([one, total - one])
    tallies = jnp.asarray(length_profile(number_of, total, bound, skew), jnp.int32)
    pairs = (number_of - 1) // 2
    giver, sink = tallies[1:1 + 2 * pairs:2], tallies[2:2 + 2 * pairs:2]
    slack = jnp.minimum(giver - 1, bound - sink)
    passed = jax.random.randint(jax.random.fold_in(stream_key, 1), (pairs,), 0, 1 << 20) % (slack + 1)
    tallies = tallies.at[1:1 + 2 * pairs:2].set(giver - passed).at[2:2 + 2 * pairs:2].set(sink + passed)
    return tallies[jax.random.permutation(jax.random.fold_in(stream_key, 2), number_of)]


def scatter_about(stream_key, extent, scale, reach, pieces=(), held_as=jnp.bfloat16):
    level = steps_of(stream_key, extent, pieces, -0.22, 0.18) if pieces else 1.0
    entries = jax.random.normal(stream_key, extent, jnp.float32) * scale * level
    return jnp.minimum(jnp.maximum(entries, -reach), reach).astype(held_as)


def setup_inputs(seed: int = 0) -> dict:
    streams_of = jax.random.split(jax.random.key(seed), 25)
    tokens = scatter_about(streams_of[0], (SEQS, LEN, D), 1.0, 6.0, ((0, 16),))
    cotangent = scatter_about(streams_of[1], (SEQS, LEN, D), 1.0, 6.0, ((0, 16),))
    image_ids = jax.vmap(lambda own: jnp.searchsorted(jnp.cumsum(ragged(own, IMG_SEQ, LEN, IMG_MOST, 0)), jnp.arange(LEN), side="right"))(jax.random.split(streams_of[2], SEQS)).reshape((SEQS, LEN)).astype(jnp.int32)
    step_rates = jnp.clip(jax.random.uniform(streams_of[3], (2,), jnp.float32, 0.2, 0.6), 0.2, 0.6)
    w_qkv = scatter_about(streams_of[4], (D, 3, D), D ** -0.5, 0.21875, ((0, 16), (2, 2)), jnp.float32)
    w_out = scatter_about(streams_of[5], (D, D), (D // 64) ** -0.5, 1.75, ((0, 2), (1, 16)), jnp.float32)
    w_up = scatter_about(streams_of[6], (D, FF), (D // 4) ** -0.5, 0.4375, ((0, 16), (1, 2)), jnp.float32)
    w_down = scatter_about(streams_of[7], (FF, D), (FF // 4) ** -0.5, 0.21875, ((0, 2), (1, 16)), jnp.float32)
    norm_gains = jnp.clip(1.0 + 0.1 * jax.random.normal(streams_of[8], (2, D), jnp.float32), 0.5, 1.5)
    row_biases = scatter_about(streams_of[9], (4, D), 0.3, 1.8, (), jnp.float32)
    head_gains = jnp.clip(1.0 + 0.1 * jax.random.normal(streams_of[10], (2, DH), jnp.float32), 0.5, 1.5)
    query_bias = scatter_about(streams_of[11], (DH,), 0.3, 1.8, (), jnp.float32)
    qkv_bias = scatter_about(streams_of[12], (3, D), 0.3, 1.8, ((1, 2),), jnp.float32)
    hidden_bias = scatter_about(streams_of[13], (FF,), 0.3, 1.8, ((0, 2),), jnp.float32)
    mom_qkv = scatter_about(streams_of[14], (D, 3, D), (0.5 * TOKENS ** 0.5), 384.0, ((0, 16), (2, 2)), jnp.float32)
    mom_out = draw_mom_out(jax.random.fold_in(streams_of[24], 71), 0)
    mom_up = scatter_about(streams_of[16], (D, FF), (0.5 * TOKENS ** 0.5), 384.0, ((0, 16), (1, 2)), jnp.float32)
    mom_down = scatter_about(streams_of[17], (FF, D), (0.5 * TOKENS ** 0.5), 384.0, ((0, 2), (1, 16)), jnp.float32)
    mom_gains = scatter_about(streams_of[18], (2, D), (1.5 * TOKENS ** 0.5), 1024.0, (), jnp.float32)
    mom_biases = scatter_about(streams_of[19], (4, D), (2.0 * TOKENS ** 0.5), 1536.0, (), jnp.float32)
    mom_head_gains = scatter_about(streams_of[20], (2, DH), (3.0 * TOKENS ** 0.5), 2048.0, (), jnp.float32)
    mom_query_bias = scatter_about(streams_of[21], (DH,), (4.0 * TOKENS ** 0.5), 3072.0, (), jnp.float32)
    mom_qkv_bias = scatter_about(streams_of[22], (3, D), (2.0 * TOKENS ** 0.5), 1536.0, ((1, 2),), jnp.float32)
    mom_hidden_bias = scatter_about(streams_of[23], (FF,), (0.5 * TOKENS ** 0.5), 384.0, ((0, 2),), jnp.float32)
    return dict(tokens=tokens, cotangent=cotangent, image_ids=image_ids, step_rates=step_rates, w_qkv=w_qkv, w_out=w_out, w_up=w_up, w_down=w_down, norm_gains=norm_gains, row_biases=row_biases, head_gains=head_gains, query_bias=query_bias, qkv_bias=qkv_bias, hidden_bias=hidden_bias, mom_qkv=mom_qkv, mom_out=mom_out, mom_up=mom_up, mom_down=mom_down, mom_gains=mom_gains, mom_biases=mom_biases, mom_head_gains=mom_head_gains, mom_query_bias=mom_query_bias, mom_qkv_bias=mom_qkv_bias, mom_hidden_bias=mom_hidden_bias)


EPS = 1e-06
NS_A = 3.4445
NS_B = -4.775
NS_C = 2.0315
HIGHEST = lax.Precision.HIGHEST

@jax.custom_vjp
def low(v):
    return lax.optimization_barrier(v.astype(jnp.bfloat16)).astype(jnp.float32)

@jax.custom_vjp
def low_back(v):
    return v

def low_keep(v):
    return (low(v), None)

def low_pass(kept, grad):
    return (grad,)

def back_keep(v):
    return (v, None)

def back_low(kept, grad):
    return (low(grad),)
low.defvjp(low_keep, low_pass)
low_back.defvjp(back_keep, back_low)

def layer_norm(values_in, gain_row, shift_row):
    row_mean = lax.optimization_barrier(jnp.mean(values_in, axis=-1, keepdims=True))
    centred = values_in - row_mean
    row_var = lax.optimization_barrier(jnp.mean(centred * centred, axis=-1, keepdims=True))
    return centred * lax.rsqrt(row_var + EPS) * gain_row + shift_row

def gelu_tanh(values_in):
    return jax.nn.gelu(values_in, approximate=True)

def attend_one(seq_item):
    query_in, keys_in, values, image_row = seq_item
    scores = low_back(jnp.einsum('qhd,khd->hqk', query_in, keys_in, precision=HIGHEST))
    same_image = image_row[:, None] == image_row[None, :]
    scores = jnp.where(same_image[None], scores, -1000000000.0)
    row_total = jax.nn.logsumexp(scores, axis=-1, keepdims=True)
    attn_probs = low(jnp.exp(scores - row_total))
    return jnp.einsum('hqk,khd->qhd', attn_probs, values, precision=HIGHEST)

def group_forward(params, x_group, id_group):
    w_qkv, w_out, w_up, w_down, norm_gains, row_biases, head_gains, query_bias, qkv_bias, hidden_bias = params
    seq_total = x_group.shape[0]
    row_count = seq_total * LEN
    flat_in = x_group.reshape(row_count, D)
    normed = low(layer_norm(flat_in, norm_gains[0], row_biases[0]))
    half_width = D // N_TENSOR
    heads_part = half_width // DH
    attn_out = row_biases[1]
    for head_group in range(N_TENSOR):
        col_range = slice(head_group * half_width, (head_group + 1) * half_width)
        w_part = low(w_qkv[:, :, col_range]).reshape(D, 3 * half_width)
        raw_qkv = low_back(jnp.dot(normed, w_part, precision=HIGHEST))
        raw_qkv = (raw_qkv + qkv_bias[:, col_range].reshape(3 * half_width)).reshape(row_count, 3, heads_part, DH)
        query_low = low(layer_norm(raw_qkv[:, 0], head_gains[0], query_bias) * DH ** (-0.5))
        keys_low = low(layer_norm(raw_qkv[:, 1], head_gains[1], 0.0))
        values_low = low(raw_qkv[:, 2])
        seq_shape = (seq_total, LEN, heads_part, DH)
        mixed_heads = lax.map(jax.checkpoint(attend_one), (query_low.reshape(seq_shape), keys_low.reshape(seq_shape), values_low.reshape(seq_shape), id_group))
        mixed_heads = low(low_back(mixed_heads.reshape(row_count, half_width)))
        attn_out = attn_out + low_back(jnp.dot(mixed_heads, low(w_out[col_range, :]), precision=HIGHEST))
    residual = flat_in + attn_out
    normed_two = low(layer_norm(residual, norm_gains[1], row_biases[2]))
    hidden_part = FF // N_TENSOR
    mlp_out = row_biases[3]
    for head_group in range(N_TENSOR):
        col_range = slice(head_group * hidden_part, (head_group + 1) * hidden_part)
        pre_act = low_back(jnp.dot(normed_two, low(w_up[:, col_range]), precision=HIGHEST)) + hidden_bias[col_range]
        act_out = low(gelu_tanh(pre_act))
        mlp_out = mlp_out + low_back(jnp.dot(act_out, low(w_down[col_range, :]), precision=HIGHEST))
    return (residual + mlp_out).reshape(seq_total, LEN, D)

def orthogonalize(matrix):
    iterate = matrix
    for turn in range(NS_ITERS):
        gram_matrix = jnp.dot(iterate, iterate.T, precision=HIGHEST)
        if turn == 0:
            root = jnp.sqrt(jnp.trace(gram_matrix)) + 1e-07
            gram_matrix = gram_matrix / (root * root)
        poly_term = NS_B * gram_matrix + NS_C * jnp.dot(gram_matrix, gram_matrix, precision=HIGHEST)
        iterate = NS_A * iterate + jnp.dot(poly_term, iterate, precision=HIGHEST)
        if turn == 0:
            iterate = iterate / root
    return iterate

def reference(tokens, cotangent, image_ids, step_rates, w_qkv, w_out, w_up, w_down, norm_gains, row_biases, head_gains, query_bias, qkv_bias, hidden_bias, mom_qkv, mom_out, mom_up, mom_down, mom_gains, mom_biases, mom_head_gains, mom_query_bias, mom_qkv_bias, mom_hidden_bias):
    params = (w_qkv, w_out, w_up, w_down, norm_gains, row_biases, head_gains, query_bias, qkv_bias, hidden_bias)
    moments = (mom_qkv, mom_out, mom_up, mom_down, mom_gains, mom_biases, mom_head_gains, mom_query_bias, mom_qkv_bias, mom_hidden_bias)
    group_seqs = 4
    group_count = SEQS // group_seqs
    id_groups = image_ids.reshape(group_count, group_seqs, LEN)

    def forward(weights, inputs_f):

        def one_group(seq_group):
            return group_forward(weights, seq_group[0], seq_group[1])
        outputs = lax.map(jax.checkpoint(one_group), (inputs_f.reshape(group_count, group_seqs, LEN, D), id_groups))
        return outputs.reshape(SEQS, LEN, D)
    block_y, pullback = jax.vjp(forward, params, tokens.astype(jnp.float32))
    gradients, tokens_grad = pullback(cotangent.astype(jnp.float32))
    next_moms = [0.5 * mom_item + grad_item for mom_item, grad_item in zip(moments, gradients)]
    matrices = [next_moms[0].reshape(D, 3 * D), next_moms[1].T, next_moms[2], next_moms[3].T]
    updates = []
    for matrix in matrices:
        factor = 0.2 * math.sqrt(max(matrix.shape[0], matrix.shape[1]))
        updates.append(step_rates[0] * factor * orthogonalize(matrix))
    new_w_qkv = w_qkv - updates[0].reshape(D, 3, D)
    new_w_out = w_out - updates[1].T
    new_w_up = w_up - updates[2]
    new_w_down = w_down - updates[3].T
    rate_vector = step_rates[1] / math.sqrt(TOKENS)
    new_vectors = [param_item - rate_vector * mom_item for param_item, mom_item in zip(params[4:], next_moms[4:])]
    return (block_y, tokens_grad, gradients[0], gradients[1], gradients[2], gradients[3], gradients[4], gradients[5], gradients[6], gradients[7], gradients[8], gradients[9], next_moms[0], next_moms[1], next_moms[2], next_moms[3], next_moms[4], next_moms[5], next_moms[6], next_moms[7], next_moms[8], next_moms[9], new_w_qkv, new_w_out, new_w_up, new_w_down, new_vectors[0], new_vectors[1], new_vectors[2], new_vectors[3], new_vectors[4], new_vectors[5])
```

```python
import functools
import math

import jax
import jax.numpy as jnp
from jax import lax
from jax.experimental import pallas as pl
from jax.experimental.pallas import tpu as pltpu
from jax.sharding import PartitionSpec as P

D = 768
DH = 64
FF = 3072
NS_ITERS = 5


EPS = 1e-06
NS_A = 3.4445
NS_B = -4.775
NS_C = 2.0315
BF = jnp.bfloat16
F32 = jnp.float32
BOTH = ("dp", "tensor")


def exchange(block, flip_zero, flip_one):
    pairs = []
    for place in range(lax.axis_size("dp")):
        for core, flip in enumerate((flip_zero, flip_one)):
            pairs.append((2 * place + core, 2 * (place ^ flip) + core))
    return lax.ppermute(block, BOTH, pairs)


def swap_cores(block):
    return lax.ppermute(block, "tensor", [(0, 1), (1, 0)])


def pick(stack, index):
    return lax.dynamic_index_in_dim(stack, index, 0, keepdims=False)


def gather_rows(block):
    if lax.axis_size("dp") != 16:
        return lax.all_gather(block, "dp", axis=0, tiled=True)
    rows, columns = block.shape
    place = lax.axis_index("dp")
    inner, outer = place % 4, place // 4
    first = lax.axis_index("tensor") == 0
    pieces = jnp.stack([block] + [exchange(block, 4 * d, 4 * d) for d in (1, 2, 3)])
    own = jnp.stack([pick(pieces, outer ^ d) for d in range(4)])
    turned = exchange(own, 2, 1)
    both = exchange(jnp.stack([own, turned]), 1, 2)
    flip_one = jnp.where(first, both[0], turned)
    flip_two = jnp.where(first, turned, both[0])
    groups = jnp.stack([own, flip_one, flip_two, both[1]])
    placed = jnp.stack([pick(groups, inner ^ j) for j in range(4)], axis=1)
    return placed.reshape(16 * rows, columns)


def scatter_sum(whole):
    count = lax.axis_size("dp")
    if count != 16:
        return lax.psum_scatter(whole, "dp", scatter_dimension=0, tiled=True)
    rows, columns = whole.shape[0] // count, whole.shape[1]
    place = lax.axis_index("dp")
    inner, outer = place % 4, place // 4
    first = lax.axis_index("tensor") == 0
    near = jnp.where(first, 2, 1)
    groups = whole.reshape(4, 4, rows, columns)

    def group(flip):
        return lax.dynamic_index_in_dim(groups, inner ^ flip, 1, keepdims=False)

    sent = exchange(jnp.stack([group(near), group(3)]).astype(BF), 2, 1).astype(F32)
    sent_two = exchange((group(3 - near) + sent[1]).astype(BF), 1, 2).astype(F32)
    plane = group(0) + sent[0] + sent_two
    total = pick(plane, outer)
    arrived = [exchange(pick(plane, outer ^ d).astype(BF), 4 * d, 4 * d) for d in (1, 2, 3)]
    for part in arrived:
        total = total + part.astype(F32)
    return total


def sum_everywhere(block):
    count = lax.axis_size("dp")
    if count & (count - 1):
        return lax.psum(block, "dp")
    flip = 1
    while flip < count:
        block = block + exchange(block, flip, flip)
        flip *= 2
    return block


def eye_block(first_row, rows, columns):
    row = lax.broadcasted_iota(jnp.int32, (rows, columns), 0) + first_row
    return row == lax.broadcasted_iota(jnp.int32, (rows, columns), 1)


def nn(left, right):
    return lax.dot_general(left, right, (((1,), (0,)), ((), ())), preferred_element_type=F32)


def nt(left, right):
    return lax.dot_general(left, right, (((1,), (1,)), ((), ())), preferred_element_type=F32)


def ns_kernel(x_ref, o_ref, y_ref, a_ref, ab_ref, p_ref, pb_ref, r_ref, rb_ref, col_ref, row_ref):
    blk = 256
    steps = D // blk
    columns = x_ref.shape[1]
    chunk = 768

    def put(full_ref, half_ref, slot, i, value):
        rows = pl.ds(pl.multiple_of(i * blk, blk), blk)
        eye = eye_block(i * blk, blk, D)
        only = jnp.where(eye, value, 0.0)
        full_ref[rows, :] = value
        half_ref[rows, :] = jnp.where(eye, 0.0, value).astype(BF)
        col_ref[slot, rows, :] = jnp.sum(only, axis=1, keepdims=True)
        part = jnp.sum(only, axis=0, keepdims=True)

        @pl.when(i == 0)
        def _():
            row_ref[slot] = part

        @pl.when(i > 0)
        def _():
            row_ref[slot] = row_ref[slot] + part

    def gram(src):
        def outer(i, carry):
            rows = pl.ds(pl.multiple_of(i * blk, blk), blk)

            def inner(k, carry):
                cols = pl.ds(pl.multiple_of(k * chunk, chunk), chunk)
                part = nt(src[rows, cols], src[:, cols])

                @pl.when(k == 0)
                def _():
                    r_ref[rows, :] = part

                @pl.when(k > 0)
                def _():
                    r_ref[rows, :] = r_ref[rows, :] + part

                return carry

            return lax.fori_loop(0, columns // chunk, inner, carry)

        lax.fori_loop(0, steps, outer, 0)

    def keep_gram(scale):
        def step(i, carry):
            rows = pl.ds(pl.multiple_of(i * blk, blk), blk)
            put(a_ref, ab_ref, 0, i, r_ref[rows, :] * scale)
            return carry

        lax.fori_loop(0, steps, step, 0)

    def polynomial(turn):
        def step(i, carry):
            rows = pl.ds(pl.multiple_of(i * blk, blk), blk)
            eye = eye_block(i * blk, blk, D)
            dcol, drow = col_ref[0, rows, :], row_ref[0]
            square = nn(ab_ref[rows, :], ab_ref[...])
            value = NS_C * square + a_ref[rows, :] * (NS_B + NS_C * (dcol + drow))
            value = value + jnp.where(eye, NS_A - NS_C * dcol * dcol, 0.0)
            put(p_ref, pb_ref.at[turn], 2 + turn, i, value)
            return carry

        lax.fori_loop(0, steps, step, 0)

    def times(left, left_half, lslot, right, right_half, rslot, out, out_half, oslot):
        def step(i, carry):
            rows = pl.ds(pl.multiple_of(i * blk, blk), blk)
            eye = eye_block(i * blk, blk, D)
            lcol, rrow = col_ref[lslot, rows, :], row_ref[rslot]
            value = nn(left_half[rows, :], right_half[...])
            value = value + lcol * right[rows, :] + left[rows, :] * rrow
            value = value - jnp.where(eye, lcol * rrow, 0.0)
            put(out, out_half, oslot, i, value)
            return carry

        lax.fori_loop(0, steps, step, 0)

    gram(x_ref)

    def trace_step(i, total):
        rows = pl.ds(pl.multiple_of(i * blk, blk), blk)
        return total + jnp.sum(jnp.where(eye_block(i * blk, blk, D), r_ref[rows, :], 0.0))

    trace = lax.fori_loop(0, steps, trace_step, jnp.float32(0.0))
    root = jnp.sqrt(jnp.full((1, 1), trace, F32)) + 1e-07
    keep_gram(1.0 / (root * root))
    polynomial(0)
    inverse = 1.0 / root

    def apply_outer(i, carry):
        rows = pl.ds(pl.multiple_of(i * blk, blk), blk)

        def apply_inner(k, carry):
            cols = pl.ds(pl.multiple_of(k * chunk, chunk), chunk)
            value = nn(pb_ref[0, rows, :], x_ref[:, cols])
            value = value + col_ref[2, rows, :] * x_ref[rows, cols].astype(F32)
            y_ref[rows, cols] = (value * inverse).astype(BF)
            return carry

        return lax.fori_loop(0, columns // chunk, apply_inner, carry)

    lax.fori_loop(0, steps, apply_outer, 0)
    gram(y_ref)
    keep_gram(1.0)

    def turn_body(turn, carry):
        polynomial(turn)
        times(p_ref, pb_ref.at[turn], 2 + turn, a_ref, ab_ref, 0, r_ref, rb_ref, 1)
        times(r_ref, rb_ref, 1, p_ref, pb_ref.at[turn], 2 + turn, a_ref, ab_ref, 0)
        return carry

    lax.fori_loop(1, NS_ITERS - 1, turn_body, 0)
    polynomial(NS_ITERS - 1)

    wanted = o_ref.shape[0]
    eye = eye_block(0, wanted, D)
    r_ref[:wanted, :] = p_ref[:wanted, :]

    def chain(step, carry):
        turn = NS_ITERS - 2 - step
        left = r_ref[:wanted, :]
        only = jnp.where(eye, left, 0.0)
        lcol = jnp.sum(only, axis=1, keepdims=True)
        off = left - only
        right_half = pb_ref[turn]
        drow = row_ref[2 + turn]
        value = nn(off.astype(BF), right_half)
        value = value + lcol * right_half[:wanted, :].astype(F32) + left * drow
        r_ref[:wanted, :] = value
        return carry

    lax.fori_loop(0, NS_ITERS - 2, chain, 0)
    left = r_ref[:wanted, :]
    only = jnp.where(eye, left, 0.0)
    lcol = jnp.sum(only, axis=1, keepdims=True)
    off = (left - only).astype(BF)
    kept = o_ref.shape[1]
    for k in range(kept // chunk):
        cols = slice(k * chunk, (k + 1) * chunk)
        value = nn(off, y_ref[:, cols]) + lcol * y_ref[:wanted, cols].astype(F32)
        o_ref[:, cols] = value.astype(BF)


def orthogonal_rows(matrix, wanted, kept):
    vmem = pl.BlockSpec(memory_space=pltpu.VMEM)
    return pl.pallas_call(
        ns_kernel,
        out_shape=jax.ShapeDtypeStruct((wanted, kept), BF),
        in_specs=[vmem],
        out_specs=vmem,
        scratch_shapes=[
            pltpu.VMEM(matrix.shape, BF),
            pltpu.VMEM((D, D), F32),
            pltpu.VMEM((D, D), BF),
            pltpu.VMEM((D, D), F32),
            pltpu.VMEM((NS_ITERS, D, D), BF),
            pltpu.VMEM((D, D), F32),
            pltpu.VMEM((D, D), BF),
            pltpu.VMEM((2 + NS_ITERS, D, 1), F32),
            pltpu.VMEM((2 + NS_ITERS, 1, D), F32),
        ],
        compiler_params=pltpu.CompilerParams(vmem_limit_bytes=60 * 1024 * 1024),
        cost_estimate=pl.CostEstimate(flops=30 * D**3 * 2, bytes_accessed=2 * matrix.size, transcendentals=0),
        name="newton_schulz",
    )(matrix)


def own_matrix(packed, starts, widths):
    place = lax.axis_index("dp")
    rows = packed.shape[0]
    widest = max(widths)
    start = jnp.array(starts, jnp.int32)
    width = jnp.array(widths, jnp.int32)
    spare = max(0, starts[-1] + widest - packed.shape[1], max(starts) + widest - packed.shape[1])
    packed = jnp.pad(packed, ((0, 0), (0, spare)))
    inner = place % 4

    def columns_of(whole, which):
        return lax.dynamic_slice_in_dim(whole, pick(start, which), widest, whole.ndim - 1)

    if lax.axis_size("dp") == 16:
        planes = jnp.stack([packed] + [exchange(packed, 4 * d, 4 * d) for d in (1, 2, 3)])
        mine = [columns_of(planes, inner)]
        for d in (1, 2, 3):
            mine.append(exchange(columns_of(planes, inner ^ d), d, d))
        whole = jnp.stack(mine, axis=1).reshape(16 * rows, widest)
    else:
        whole = lax.all_gather(packed, "dp", axis=0, tiled=True)
        whole = columns_of(whole, inner)
        count = lax.axis_size("dp")
        turn = (jnp.arange(count) + place // 4 * 4) % count
        turn = jnp.concatenate([turn[:4][jnp.arange(4) ^ inner], turn[4:]])
        whole = whole.reshape(count, rows, widest)[turn].reshape(count * rows, widest)
    whole = jnp.where(jnp.arange(widest) < pick(width, inner), whole, jnp.zeros_like(whole))
    return jnp.concatenate([whole, swap_cores(whole)], axis=1)


def rows_of_all(block, rows):
    inner = lax.axis_index("dp") % 4
    parts = [block[:rows]]
    for d in (1, 2, 3):
        parts.append(exchange(block[d * rows : (d + 1) * rows], d, d))
    parts = jnp.stack(parts)
    return [pick(parts, inner ^ j).astype(F32) for j in range(4)]


def layer_norm(values_in, gain_row, shift_row):
    row_mean = jnp.mean(values_in, axis=-1, keepdims=True)
    centred = values_in - row_mean
    row_var = jnp.mean(centred * centred, axis=-1, keepdims=True)
    return centred * lax.rsqrt(row_var + EPS) * gain_row + shift_row


def gelu_tanh(values_in):
    return jax.nn.gelu(values_in, approximate=True)


def project_heads(raw_query, raw_keys, head_gains, query_bias):
    query_out = layer_norm(raw_query, head_gains[0], query_bias) * DH ** (-0.5)
    keys_out = layer_norm(raw_keys, head_gains[1], 0.0)
    return (query_out, keys_out)


def dense(left_in, right_in):
    return jnp.dot(left_in, right_in, preferred_element_type=jnp.float32)


def dense_tn(left_in, right_in):
    return lax.dot_general(
        left_in, right_in, (((0,), (0,)), ((), ())), preferred_element_type=jnp.float32
    )


def dense_nt(left_in, right_in):
    return lax.dot_general(
        left_in, right_in, (((1,), (1,)), ((), ())), preferred_element_type=jnp.float32
    )


def masked_scores(query_rows, keys_in, image_row, first_row, block_rows):
    scores = jnp.einsum("qhd,khd->hqk", query_rows, keys_in, preferred_element_type=jnp.float32)
    same_image = image_row[first_row : first_row + block_rows, None] == image_row[None, :]
    return jnp.where(same_image[None], scores, -1000000000.0)


def attend_forward(seq_item):
    query_in, keys_in, values, image_row = seq_item
    length = query_in.shape[0]
    block_rows = min(512, length)
    outputs = []
    totals = []
    for first_row in range(0, length, block_rows):
        scores = masked_scores(
            query_in[first_row : first_row + block_rows], keys_in, image_row, first_row, block_rows
        )
        row_max = jnp.max(scores, axis=-1, keepdims=True)
        row_total = row_max + jnp.log(jnp.sum(jnp.exp(scores - row_max), axis=-1, keepdims=True))
        attn_probs = jnp.exp(scores - row_total).astype(jnp.bfloat16)
        outputs.append(
            jnp.einsum("hqk,khd->qhd", attn_probs, values, preferred_element_type=jnp.float32)
        )
        totals.append(row_total)
    return (jnp.concatenate(outputs, 0), jnp.concatenate(totals, 1))


def attend_backward(seq_item):
    query_in, keys_in, values, image_row, totals, grad_mixed = seq_item
    length = query_in.shape[0]
    block_rows = min(512, length)
    grad_query_parts = []
    grad_keys = jnp.zeros(keys_in.shape, jnp.float32)
    grad_values = jnp.zeros(values.shape, jnp.float32)
    for first_row in range(0, length, block_rows):
        query_rows = query_in[first_row : first_row + block_rows]
        grad_rows = grad_mixed[first_row : first_row + block_rows]
        scores = masked_scores(query_rows, keys_in, image_row, first_row, block_rows)
        attn_probs = jnp.exp(scores - totals[:, first_row : first_row + block_rows])
        grad_probs = jnp.einsum(
            "qhd,khd->hqk", grad_rows, values, preferred_element_type=jnp.float32
        )
        grad_scores = attn_probs * (
            grad_probs - jnp.sum(grad_probs * attn_probs, axis=-1, keepdims=True)
        )
        grad_scores = grad_scores.astype(jnp.bfloat16)
        grad_query_parts.append(
            jnp.einsum("hqk,khd->qhd", grad_scores, keys_in, preferred_element_type=jnp.float32)
        )
        grad_keys = grad_keys + jnp.einsum(
            "hqk,qhd->khd", grad_scores, query_rows, preferred_element_type=jnp.float32
        )
        grad_values = grad_values + jnp.einsum(
            "hqk,qhd->khd",
            attn_probs.astype(jnp.bfloat16),
            grad_rows,
            preferred_element_type=jnp.float32,
        )
    return (jnp.concatenate(grad_query_parts, 0), grad_keys, grad_values)


def body(
    tokens,
    cotangent,
    image_ids,
    step_rates,
    w_qkv,
    w_out,
    w_up,
    w_down,
    norm_gains,
    row_biases,
    head_gains,
    query_bias,
    qkv_bias,
    hidden_bias,
    mom_qkv,
    mom_out,
    mom_up,
    mom_down,
    mom_gains,
    mom_biases,
    mom_head_gains,
    mom_query_bias,
    mom_qkv_bias,
    mom_hidden_bias,
):
    dp_count = lax.axis_size("dp")
    seq_count, length, model_width = tokens.shape
    row_count = seq_count * length
    shard_rows = w_qkv.shape[0]
    half_width = w_qkv.shape[2]
    hidden_part = w_up.shape[1]
    heads_part = half_width // DH
    widths = [3 * half_width, half_width, hidden_part, hidden_part]
    starts = [0, widths[0], widths[0] + widths[1], widths[0] + widths[1] + widths[2]]
    low_weights = jnp.concatenate(
        [w_qkv.reshape(shard_rows, 3 * half_width), w_out.T, w_up, w_down.T], axis=1
    ).astype(BF)
    first_weights = gather_rows(low_weights[:, : starts[2]])
    last_weights = lax.all_gather(low_weights[:, starts[2] :], "dp", axis=0, tiled=True)
    qkv_matrix, out_rows = first_weights[:, : starts[1]], first_weights[:, starts[1] :]
    full_up, down_rows = last_weights[:, :hidden_part], last_weights[:, hidden_part:]
    flat_in = tokens.reshape(row_count, model_width).astype(jnp.float32)
    normed_f, norm_one_pull = jax.vjp(layer_norm, flat_in, norm_gains[0], row_biases[0])
    normed_one = normed_f.astype(jnp.bfloat16)
    raw_qkv = dense(normed_one, qkv_matrix) + qkv_bias.reshape(3 * half_width)
    raw_qkv = raw_qkv.reshape(row_count, 3, heads_part, DH)
    (query_f, keys_f), head_pull = jax.vjp(
        project_heads, raw_qkv[:, 0], raw_qkv[:, 1], head_gains, query_bias
    )
    seq_shape = (seq_count, length, heads_part, DH)
    query_low = query_f.astype(jnp.bfloat16).reshape(seq_shape)
    keys_low = keys_f.astype(jnp.bfloat16).reshape(seq_shape)
    values_low = raw_qkv[:, 2].astype(jnp.bfloat16).reshape(seq_shape)
    mixed_f, totals = lax.map(attend_forward, (query_low, keys_low, values_low, image_ids))
    mixed_heads = mixed_f.reshape(row_count, half_width).astype(jnp.bfloat16)
    attn_part = dense_nt(mixed_heads, out_rows).astype(BF)
    attn_out = attn_part.astype(F32) + swap_cores(attn_part).astype(F32) + row_biases[1]
    residual = flat_in + attn_out
    normed_two_f, norm_two_pull = jax.vjp(layer_norm, residual, norm_gains[1], row_biases[2])
    normed_two = normed_two_f.astype(jnp.bfloat16)
    pre_act = dense(normed_two, full_up) + hidden_bias
    act_f, gelu_pull = jax.vjp(gelu_tanh, pre_act)
    act_out = act_f.astype(jnp.bfloat16)
    mlp_part = dense_nt(act_out, down_rows).astype(BF)
    mlp_out = mlp_part.astype(F32) + swap_cores(mlp_part).astype(F32) + row_biases[3]
    block_out = (residual + mlp_out).reshape(tokens.shape)
    grad_y = cotangent.reshape(row_count, model_width).astype(jnp.float32)
    grad_y_low = grad_y.astype(jnp.bfloat16)
    grad_down_local = dense_tn(grad_y_low, act_out)
    (grad_pre,) = gelu_pull(dense(grad_y_low, down_rows))
    grad_pre_low = grad_pre.astype(jnp.bfloat16)
    grad_up_local = dense_tn(normed_two, grad_pre_low)
    part_two = dense_nt(grad_pre_low, full_up).astype(BF)
    grad_normed_two = part_two.astype(F32) + swap_cores(part_two).astype(F32)
    late = scatter_sum(jnp.concatenate([grad_up_local, grad_down_local], axis=1))
    grad_resid_ln, grad_gain_two, grad_shift_two = norm_two_pull(grad_normed_two)
    grad_resid = grad_y + grad_resid_ln
    grad_resid_low = grad_resid.astype(jnp.bfloat16)
    grad_out_local = dense_tn(grad_resid_low, mixed_heads)
    grad_mixed = dense(grad_resid_low, out_rows).astype(jnp.bfloat16).reshape(seq_shape)
    grad_query, grad_keys, grad_values = lax.map(
        attend_backward, (query_low, keys_low, values_low, image_ids, totals, grad_mixed)
    )
    head_shape = (row_count, heads_part, DH)
    grad_raw_query, grad_raw_keys, grad_head_local, grad_qshift_local = head_pull(
        (grad_query.reshape(head_shape), grad_keys.reshape(head_shape))
    )
    grad_raw = jnp.stack(
        [grad_raw_query, grad_raw_keys, grad_values.reshape(head_shape)], axis=1
    ).reshape(row_count, 3 * half_width)
    grad_qkv_bias_local = jnp.sum(grad_raw, axis=0).reshape(3, half_width)
    grad_raw_low = grad_raw.astype(jnp.bfloat16)
    grad_qkv_local = dense_tn(normed_one, grad_raw_low)
    early = scatter_sum(jnp.concatenate([grad_qkv_local, grad_out_local], axis=1))
    part_one = dense_nt(grad_raw_low, qkv_matrix).astype(BF)
    grad_normed_one = part_one.astype(F32) + swap_cores(part_one).astype(F32)
    grad_flat_ln, grad_gain_one, grad_shift_one = norm_one_pull(grad_normed_one)
    tokens_grad = (grad_resid + grad_flat_ln).reshape(tokens.shape)
    grad_rows = [early[:, : starts[1]], early[:, starts[1] :], late[:, :hidden_part], late[:, hidden_part:]]
    grad_qkv = grad_rows[0].reshape(shard_rows, 3, half_width)
    grad_out, grad_up, grad_down = grad_rows[1].T, grad_rows[2], grad_rows[3].T
    next_mom_qkv = 0.5 * mom_qkv + grad_qkv
    next_mom_out = 0.5 * mom_out + grad_out
    next_mom_up = 0.5 * mom_up + grad_up
    next_mom_down = 0.5 * mom_down + grad_down
    packed = jnp.concatenate(
        [next_mom_qkv.reshape(shard_rows, 3 * half_width), next_mom_out.T, next_mom_up, next_mom_down.T],
        axis=1,
    ).astype(BF)
    matrix = own_matrix(packed, starts, widths)
    own_rows = rows_of_all(orthogonal_rows(matrix, 4 * shard_rows, hidden_part), shard_rows)
    small = [
        jnp.stack([grad_gain_one, grad_gain_two]),
        jnp.stack([grad_shift_one, jnp.sum(grad_resid, axis=0), grad_shift_two, jnp.sum(grad_y, axis=0)]),
        grad_qkv_bias_local,
        jnp.sum(grad_pre, axis=0),
        grad_head_local,
        grad_qshift_local,
    ]
    sizes = [part.size for part in small]
    flat = jnp.concatenate([part.reshape(-1) for part in small])
    flat = jnp.pad(flat, (0, -flat.size % 1024)).reshape(-1, 128)
    summed = sum_everywhere(flat)
    cut = sum(sizes[:4])
    summed = summed.reshape(-1)
    heads = summed[cut : cut + sizes[4] + sizes[5]]
    heads = heads + swap_cores(heads)
    pieces = []
    at = 0
    for part, size in zip(small[:4], sizes):
        pieces.append(summed[at : at + size].reshape(part.shape))
        at += size
    grad_gains, grad_biases, grad_qkv_bias, grad_hidden_bias = pieces
    grad_head_gains = heads[: sizes[4]].reshape(grad_head_local.shape)
    grad_query_bias = heads[sizes[4] :]
    rate_muon = step_rates[0]
    new_w_qkv = w_qkv - rate_muon * (0.2 * math.sqrt(max(D, 3 * D))) * own_rows[0][
        :, : 3 * half_width
    ].reshape(shard_rows, 3, half_width)
    new_w_out = w_out - rate_muon * (0.2 * math.sqrt(D)) * own_rows[1][:, :half_width].T
    new_w_up = w_up - rate_muon * (0.2 * math.sqrt(max(D, FF))) * own_rows[2][:, :hidden_part]
    new_w_down = w_down - rate_muon * (0.2 * math.sqrt(max(D, FF))) * own_rows[3][:, :hidden_part].T
    rate_vector = step_rates[1] / math.sqrt(row_count * dp_count)
    next_mom_gains = 0.5 * mom_gains + grad_gains
    next_mom_biases = 0.5 * mom_biases + grad_biases
    next_mom_head_gains = 0.5 * mom_head_gains + grad_head_gains
    next_mom_query_bias = 0.5 * mom_query_bias + grad_query_bias
    next_mom_qkv_bias = 0.5 * mom_qkv_bias + grad_qkv_bias
    next_mom_hidden_bias = 0.5 * mom_hidden_bias + grad_hidden_bias
    new_gains = norm_gains - rate_vector * next_mom_gains
    new_biases = row_biases - rate_vector * next_mom_biases
    new_head_gains = head_gains - rate_vector * next_mom_head_gains
    new_query_bias = query_bias - rate_vector * next_mom_query_bias
    new_qkv_bias = qkv_bias - rate_vector * next_mom_qkv_bias
    new_hidden_bias = hidden_bias - rate_vector * next_mom_hidden_bias
    return (
        block_out,
        tokens_grad,
        grad_qkv,
        grad_out,
        grad_up,
        grad_down,
        grad_gains,
        grad_biases,
        grad_head_gains,
        grad_query_bias,
        grad_qkv_bias,
        grad_hidden_bias,
        next_mom_qkv,
        next_mom_out,
        next_mom_up,
        next_mom_down,
        next_mom_gains,
        next_mom_biases,
        next_mom_head_gains,
        next_mom_query_bias,
        next_mom_qkv_bias,
        next_mom_hidden_bias,
        new_w_qkv,
        new_w_out,
        new_w_up,
        new_w_down,
        new_gains,
        new_biases,
        new_head_gains,
        new_query_bias,
        new_qkv_bias,
        new_hidden_bias,
    )


def solution(mesh):
    return jax.shard_map(
        body,
        mesh=mesh,
        in_specs=(
            P("dp", None, None),
            P("dp", None, None),
            P("dp", None),
            P(),
            P("dp", None, "tensor"),
            P("tensor", "dp"),
            P("dp", "tensor"),
            P("tensor", "dp"),
            P(),
            P(),
            P(),
            P(),
            P(None, "tensor"),
            P("tensor"),
            P("dp", None, "tensor"),
            P("tensor", "dp"),
            P("dp", "tensor"),
            P("tensor", "dp"),
            P(),
            P(),
            P(),
            P(),
            P(None, "tensor"),
            P("tensor"),
        ),
        out_specs=(
            P("dp", None, None),
            P("dp", None, None),
            P("dp", None, "tensor"),
            P("tensor", "dp"),
            P("dp", "tensor"),
            P("tensor", "dp"),
            P(),
            P(),
            P(),
            P(),
            P(None, "tensor"),
            P("tensor"),
            P("dp", None, "tensor"),
            P("tensor", "dp"),
            P("dp", "tensor"),
            P("tensor", "dp"),
            P(),
            P(),
            P(),
            P(),
            P(None, "tensor"),
            P("tensor"),
            P("dp", None, "tensor"),
            P("tensor", "dp"),
            P("dp", "tensor"),
            P("tensor", "dp"),
            P(),
            P(),
            P(),
            P(),
            P(None, "tensor"),
            P("tensor"),
        ),
        check_vma=False,
    )
```

```python
import functools
import math

import jax
import jax.numpy as jnp
from jax import lax
from jax.experimental import pallas as pl
from jax.experimental.pallas import tpu as pltpu
from jax.sharding import PartitionSpec as P

D = 768
DH = 64
FF = 3072
NS_ITERS = 5


EPS = 1e-06
NS_A = 3.4445
NS_B = -4.775
NS_C = 2.0315
BF = jnp.bfloat16
F32 = jnp.float32
BOTH = ("dp", "tensor")


def exchange(block, flip_zero, flip_one, wanted=None):
    pairs = []
    for place in range(lax.axis_size("dp")):
        for core, flip in enumerate((flip_zero, flip_one)):
            if wanted is None or (place ^ flip) % 4 in wanted:
                pairs.append((2 * place + core, 2 * (place ^ flip) + core))
    return lax.ppermute(block, BOTH, pairs)


def swap_cores(block):
    return lax.ppermute(block, "tensor", [(0, 1), (1, 0)])


def pick(stack, index):
    return lax.dynamic_index_in_dim(stack, index, 0, keepdims=False)


def gather_rows(block):
    if lax.axis_size("dp") != 16:
        return lax.all_gather(block, "dp", axis=0, tiled=True)
    rows, columns = block.shape
    place = lax.axis_index("dp")
    inner, outer = place % 4, place // 4
    first = lax.axis_index("tensor") == 0
    pieces = jnp.stack([block] + [exchange(block, 4 * d, 4 * d) for d in (1, 2, 3)])
    own = jnp.stack([pick(pieces, outer ^ d) for d in range(4)])
    turned = exchange(own, 2, 1)
    both = exchange(jnp.stack([own, turned]), 1, 2)
    flip_one = jnp.where(first, both[0], turned)
    flip_two = jnp.where(first, turned, both[0])
    groups = jnp.stack([own, flip_one, flip_two, both[1]])
    placed = jnp.stack([pick(groups, inner ^ j) for j in range(4)], axis=1)
    return placed.reshape(16 * rows, columns)


def scatter_order():
    if lax.axis_size("dp") != 16:
        return jnp.arange(16, dtype=jnp.int32)
    inner = lax.axis_index("dp") % 4
    near = jnp.where(lax.axis_index("tensor") == 0, 2, 1)
    flips = jnp.stack([near, near * 0 + 3, near * 0, 3 - near])
    return ((inner ^ flips)[:, None] + 4 * jnp.arange(4)[None, :]).reshape(16).astype(jnp.int32)


def whole_sum(send, keep):
    whole = jnp.concatenate([send.astype(F32), keep]).reshape(-1, send.shape[-1])
    return lax.psum_scatter(whole, "dp", scatter_dimension=0, tiled=True)


def second_parts(keep, got):
    half = keep + got.astype(F32)
    return half[4:].astype(BF), half[:4]


def plane_parts(keep, got):
    outer = lax.axis_index("dp") // 4
    plane = keep + got.astype(F32)
    return [pick(plane, outer ^ d).astype(BF) for d in (1, 2, 3)], pick(plane, outer)


def over_planes(parts):
    return [exchange(part, 4 * d, 4 * d) for d, part in zip((1, 2, 3), parts)]


def add_all(own, parts):
    for part in parts:
        own = own + part.astype(F32)
    return own


def after(value, *others):
    return lax.optimization_barrier((value, *others))[0]


def sum_everywhere(block):
    return jnp.sum(lax.all_gather(block, BOTH, axis=0).reshape(-1, 2, *block.shape), axis=0)


def eye_block(first_row, rows, columns):
    row = lax.broadcasted_iota(jnp.int32, (rows, columns), 0) + first_row
    return row == lax.broadcasted_iota(jnp.int32, (rows, columns), 1)


def nn(left, right):
    return lax.dot_general(left, right, (((1,), (0,)), ((), ())), preferred_element_type=F32)


def nt(left, right):
    return lax.dot_general(left, right, (((1,), (1,)), ((), ())), preferred_element_type=F32)


def ns_kernel(x_ref, t_ref, o_ref, y_ref, a_ref, ab_ref, p_ref, pb_ref, r_ref, rb_ref, col_ref, row_ref):
    blk = 256
    steps = D // blk
    columns = x_ref.shape[1]
    chunk = 768
    half_chunks = columns // chunk

    def put(full_ref, half_ref, slot, i, value):
        rows = pl.ds(pl.multiple_of(i * blk, blk), blk)
        eye = eye_block(i * blk, blk, D)
        only = jnp.where(eye, value, 0.0)
        full_ref[rows, :] = value
        half_ref[rows, :] = jnp.where(eye, 0.0, value).astype(BF)
        col_ref[slot, rows, :] = jnp.sum(only, axis=1, keepdims=True)
        part = jnp.sum(only, axis=0, keepdims=True)

        @pl.when(i == 0)
        def _():
            row_ref[slot] = part

        @pl.when(i > 0)
        def _():
            row_ref[slot] = row_ref[slot] + part

    def gram(sources):
        def outer(i, carry):
            rows = pl.ds(pl.multiple_of(i * blk, blk), blk)
            total = None
            for src, at in sources:
                part = nt(src[rows, at : at + chunk], src[:, at : at + chunk])
                total = part if total is None else total + part
            r_ref[rows, :] = total
            return carry

        lax.fori_loop(0, steps, outer, 0)

    def keep_gram(scale):
        def step(i, carry):
            rows = pl.ds(pl.multiple_of(i * blk, blk), blk)
            put(a_ref, ab_ref, 0, i, r_ref[rows, :] * scale)
            return carry

        lax.fori_loop(0, steps, step, 0)

    def polynomial(turn):
        def step(i, carry):
            rows = pl.ds(pl.multiple_of(i * blk, blk), blk)
            eye = eye_block(i * blk, blk, D)
            dcol, drow = col_ref[0, rows, :], row_ref[0]
            square = nn(ab_ref[rows, :], ab_ref[...])
            value = NS_C * square + a_ref[rows, :] * (NS_B + NS_C * (dcol + drow))
            value = value + jnp.where(eye, NS_A - NS_C * dcol * dcol, 0.0)
            put(p_ref, pb_ref.at[turn], 2 + turn, i, value)
            return carry

        lax.fori_loop(0, steps, step, 0)

    def times(left, left_half, lslot, right, right_half, rslot, out, out_half, oslot):
        def step(i, carry):
            rows = pl.ds(pl.multiple_of(i * blk, blk), blk)
            eye = eye_block(i * blk, blk, D)
            lcol, rrow = col_ref[lslot, rows, :], row_ref[rslot]
            value = nn(left_half[rows, :], right_half[...])
            value = value + lcol * right[rows, :] + left[rows, :] * rrow
            value = value - jnp.where(eye, lcol * rrow, 0.0)
            put(out, out_half, oslot, i, value)
            return carry

        lax.fori_loop(0, steps, step, 0)

    gram([(ref, k * chunk) for ref in (x_ref, t_ref) for k in range(half_chunks)])

    def trace_step(i, total):
        rows = pl.ds(pl.multiple_of(i * blk, blk), blk)
        return total + jnp.sum(jnp.where(eye_block(i * blk, blk, D), r_ref[rows, :], 0.0))

    trace = lax.fori_loop(0, steps, trace_step, jnp.float32(0.0))
    root = jnp.sqrt(jnp.full((1, 1), trace, F32)) + 1e-07
    keep_gram(1.0 / (root * root))
    polynomial(0)
    inverse = 1.0 / root

    def apply_step(i, carry):
        rows = pl.ds(pl.multiple_of(i * blk, blk), blk)
        for k in range(2 * half_chunks):
            src = x_ref if k < half_chunks else t_ref
            at = (k % half_chunks) * chunk
            value = nn(pb_ref[0, rows, :], src[:, at : at + chunk])
            value = value + col_ref[2, rows, :] * src[rows, at : at + chunk].astype(F32)
            y_ref[rows, k * chunk : (k + 1) * chunk] = (value * inverse).astype(BF)
        return carry

    lax.fori_loop(0, steps, apply_step, 0)
    gram([(y_ref, k * chunk) for k in range(2 * half_chunks)])
    keep_gram(1.0)

    def turn_body(turn, carry):
        polynomial(turn)
        times(p_ref, pb_ref.at[turn], 2 + turn, a_ref, ab_ref, 0, r_ref, rb_ref, 1)
        times(r_ref, rb_ref, 1, p_ref, pb_ref.at[turn], 2 + turn, a_ref, ab_ref, 0)
        return carry

    lax.fori_loop(1, NS_ITERS - 1, turn_body, 0)
    polynomial(NS_ITERS - 1)

    wanted = o_ref.shape[0]
    eye = eye_block(0, wanted, D)
    r_ref[:wanted, :] = p_ref[:wanted, :]

    def chain(step, carry):
        turn = NS_ITERS - 2 - step
        left = r_ref[:wanted, :]
        only = jnp.where(eye, left, 0.0)
        lcol = jnp.sum(only, axis=1, keepdims=True)
        off = left - only
        right_half = pb_ref[turn]
        drow = row_ref[2 + turn]
        value = nn(off.astype(BF), right_half)
        value = value + lcol * right_half[:wanted, :].astype(F32) + left * drow
        r_ref[:wanted, :] = value
        return carry

    lax.fori_loop(0, NS_ITERS - 2, chain, 0)
    left = r_ref[:wanted, :]
    only = jnp.where(eye, left, 0.0)
    lcol = jnp.sum(only, axis=1, keepdims=True)
    off = (left - only).astype(BF)
    kept = o_ref.shape[1]
    for k in range(kept // chunk):
        cols = slice(k * chunk, (k + 1) * chunk)
        value = nn(off, y_ref[:, cols]) + lcol * y_ref[:wanted, cols].astype(F32)
        o_ref[:, cols] = value.astype(BF)


def orthogonal_rows(mine, other, wanted):
    vmem = pl.BlockSpec(memory_space=pltpu.VMEM)
    columns = mine.shape[1]
    return pl.pallas_call(
        ns_kernel,
        out_shape=jax.ShapeDtypeStruct((wanted, columns), BF),
        in_specs=[vmem, vmem],
        out_specs=vmem,
        scratch_shapes=[
            pltpu.VMEM((D, 2 * columns), BF),
            pltpu.VMEM((D, D), F32),
            pltpu.VMEM((D, D), BF),
            pltpu.VMEM((D, D), F32),
            pltpu.VMEM((NS_ITERS, D, D), BF),
            pltpu.VMEM((D, D), F32),
            pltpu.VMEM((D, D), BF),
            pltpu.VMEM((2 + NS_ITERS, D, 1), F32),
            pltpu.VMEM((2 + NS_ITERS, 1, D), F32),
        ],
        compiler_params=pltpu.CompilerParams(vmem_limit_bytes=40 * 1024 * 1024),
        cost_estimate=pl.CostEstimate(flops=30 * D**3 * 2, bytes_accessed=4 * mine.size, transcendentals=0),
        name="newton_schulz",
    )(mine, other)


def plane_columns(parts, starts, wide):
    inner = lax.axis_index("dp") % 4
    wanted = [k for k in range(4) if starts[k] is not None]
    table = jnp.array([0 if at is None else at for at in starts], jnp.int32)
    stacked = jnp.stack(parts)

    def columns_of(which):
        return lax.dynamic_slice_in_dim(stacked, pick(table, which), wide, 2)

    return [columns_of(inner)] + [exchange(columns_of(inner ^ d), d, d, wanted) for d in (1, 2, 3)]


def own_matrix(first, last, widths):
    inner = lax.axis_index("dp") % 4
    rows = first[0].shape[0]
    early_wide, late_wide = widths[0], widths[2]
    if lax.axis_size("dp") == 16:
        early = plane_columns(first, [0, widths[1], None, None], early_wide)
        late = plane_columns(last, [None, None, 0, late_wide], late_wide)
        early, late = jnp.stack(early, axis=1), jnp.stack(late, axis=1)
    else:
        count = lax.axis_size("dp")
        turn = (jnp.arange(count) + lax.axis_index("dp") // 4 * 4) % count
        turn = jnp.concatenate([turn[:4][jnp.arange(4) ^ inner], turn[4:]])
        early = lax.all_gather(first[0], "dp")[turn]
        late = lax.all_gather(last[0], "dp")[turn]
        early = lax.dynamic_slice_in_dim(early, (inner & 1) * widths[1], early_wide, 2)
        late = lax.dynamic_slice_in_dim(late, (inner & 1) * late_wide, late_wide, 2)
    column = jnp.arange(early_wide)
    early = jnp.where((inner == 0) | (column >= early_wide - widths[1]), early, jnp.zeros_like(early))
    early = early.reshape(-1, early_wide)
    early = jnp.pad(early, ((0, 0), (0, late_wide - early_wide)))
    return jnp.where(inner < 2, early, late.reshape(-1, late_wide))


def rows_of_all(block, rows):
    inner = lax.axis_index("dp") % 4
    parts = [block[:rows]]
    for d in (1, 2, 3):
        parts.append(exchange(block[d * rows : (d + 1) * rows], d, d))
    parts = jnp.stack(parts)
    return [pick(parts, inner ^ j).astype(F32) for j in range(4)]


def layer_norm(values_in, gain_row, shift_row):
    row_mean = jnp.mean(values_in, axis=-1, keepdims=True)
    centred = values_in - row_mean
    row_var = jnp.mean(centred * centred, axis=-1, keepdims=True)
    return centred * lax.rsqrt(row_var + EPS) * gain_row + shift_row


QB = 256


def tn(left, right):
    return lax.dot_general(left, right, (((0,), (0,)), ((), ())), preferred_element_type=F32)


def rows_at(i):
    return pl.ds(pl.multiple_of(i * QB, QB), QB)


def lanes_at(h):
    return pl.ds(pl.multiple_of(h * 128, 128), 128)


def centre(v):
    c = v - jnp.mean(v, axis=-1, keepdims=True)
    return c, lax.rsqrt(jnp.mean(c * c, axis=-1, keepdims=True) + EPS)


def head_blocks(value, swapped=False):
    a = lax.broadcasted_iota(jnp.int32, (128, 128), 0) // DH
    b = lax.broadcasted_iota(jnp.int32, (128, 128), 1) // DH
    return jnp.where((a != b) if swapped else (a == b), value, 0.0).astype(BF)


def spread(v, blocks):
    high = v.astype(BF)
    low = (v - high.astype(F32)).astype(BF)
    return nn(high, blocks) + nn(low, blocks)


def three_parts(v, lane, first):
    high = v.astype(BF).astype(F32)
    rest = v - high
    low = rest.astype(BF).astype(F32)
    last = rest - low
    return jnp.where(lane == first, high, jnp.where(lane == first + 1, low, last))


def forward_kernel(bounds, x_ref, w_ref, ln_ref, qb_ref, hd_ref, fq_ref, fk_ref,
                   a_ref, qa_ref, ka_ref, va_ref, ob_ref, xh_ref, rs_ref, part_ref, acc_ref):
    half = w_ref.shape[1] // 4
    pairs = half // 128
    blocks = x_ref.shape[0] // QB

    def project(i, carry):
        rows = rows_at(i)
        centred, scale = centre(x_ref[rows, :].astype(F32))
        low = (centred * scale * ln_ref[0:1, :] + ln_ref[1:2, :]).astype(BF)
        a_ref[rows, :] = low
        lane = lax.broadcasted_iota(jnp.int32, (QB, 128), 1)
        mean_blocks = head_blocks(1.0 / DH)
        fq, fk = fq_ref[rows, :].astype(F32), fk_ref[rows, :].astype(F32)
        for t in range(2 * pairs):
            cols = slice(128 * t, 128 * (t + 1))
            raw = nn(low, w_ref[:, cols]) + qb_ref[:, cols]
            raw = raw - spread(raw, mean_blocks)
            scale = lax.rsqrt(spread(raw * raw, mean_blocks) + EPS)
            normal = raw * scale
            xh_ref[rows, cols] = normal.astype(BF)
            rs_ref[rows, cols] = scale.astype(BF)
            out = normal * hd_ref[0:1, cols] + hd_ref[1:2, cols]
            extra, dst, p = (fq, qa_ref, t) if t < pairs else (fk, ka_ref, t - pairs)
            dst[rows, 256 * p : 256 * p + 128] = jnp.where(lane < DH, out, extra).astype(BF)
            dst[rows, 256 * p + 128 : 256 * p + 256] = jnp.where(lane < DH, extra, out).astype(BF)
        for p in range(pairs):
            cols = slice(2 * half + 128 * p, 2 * half + 128 * (p + 1))
            value = nn(low, w_ref[:, cols]) + qb_ref[:, cols]
            va_ref[rows, 256 * p : 256 * p + 128] = jnp.where(lane < DH, value, 1.0).astype(BF)
            va_ref[rows, 256 * p + 128 : 256 * p + 256] = jnp.where(lane < DH, 1.0, value).astype(BF)
        return carry

    lax.fori_loop(0, blocks, project, 0)

    def attend(i, carry):
        rows = rows_at(i)
        acc_ref[...] = jnp.zeros_like(acc_ref)

        def keys(j, carry):
            krows = rows_at(j)
            for h in range(2 * pairs):
                cols = slice(128 * h, 128 * (h + 1))
                weight = jnp.exp(nt(qa_ref[rows, cols], ka_ref[krows, cols])).astype(BF)
                acc_ref[:, cols] = acc_ref[:, cols] + nn(weight, va_ref[krows, cols])
            return carry

        lax.fori_loop(bounds[0, i], bounds[1, i], keys, 0)
        lane = lax.broadcasted_iota(jnp.int32, (QB, 128), 1)
        local = lane % DH
        for p in range(pairs):
            parts = []
            for k in range(2):
                cols = slice(256 * p + 128 * k, 256 * p + 128 * (k + 1))
                acc = acc_ref[:, cols]
                parts.append(acc / pltpu.roll(acc, DH, 1))
                total = three_parts(jnp.log(acc), local, 5)
                other = (lane >= DH) if k == 0 else (lane < DH)
                slot = other & (local >= 5) & (local < 8)
                qa_ref[rows, cols] = jnp.where(slot, total, qa_ref[rows, cols].astype(F32)).astype(BF)
            ob_ref[rows, 128 * p : 128 * (p + 1)] = jnp.where(lane < DH, parts[0], parts[1]).astype(BF)
        part_ref[rows, :] = nt(ob_ref[rows, :], w_ref[:, 3 * half :]).astype(BF)
        return carry

    lax.fori_loop(0, blocks, attend, 0)


def split_rows(order, full_ref, cols, send_ref, keep_ref):
    rows = full_ref.shape[0] // 16

    def move(k, carry):
        src = pl.ds(pl.multiple_of(order[k] * rows, 16), rows)
        send_ref[k, :, cols] = full_ref[src, :].astype(BF)
        src = pl.ds(pl.multiple_of(order[k + 8] * rows, 16), rows)
        keep_ref[k, :, cols] = full_ref[src, :]
        return carry

    lax.fori_loop(0, 8, move, 0)


def long_tn(left_ref, right_ref, out_ref):
    columns = right_ref.shape[1]
    chunk = 384

    def outer(i, carry):
        def inner(k, carry):
            cols = pl.ds(pl.multiple_of(k * chunk, 128), chunk)
            out_ref[rows_at(i), cols] = tn(left_ref[:, rows_at(i)], right_ref[:, cols])
            return carry

        return lax.fori_loop(0, columns // chunk, inner, carry)

    lax.fori_loop(0, left_ref.shape[1] // QB, outer, 0)


def mlp_kernel(order, x_ref, own_ref, got_ref, w_ref, hb_ref, ln_ref, gy_ref,
               h_ref, m_ref, gn_ref, gb_ref, send_ref, keep_ref, a_ref, act_ref, gp_ref, full_ref):
    hidden = w_ref.shape[1] // 2
    chunk = hidden // 2
    blocks = x_ref.shape[0] // QB
    gb_ref[...] = jnp.zeros_like(gb_ref)

    def block(i, carry):
        rows = rows_at(i)
        resid = x_ref[rows, :].astype(F32) + (own_ref[rows, :].astype(F32) + got_ref[rows, :].astype(F32))
        resid = resid + ln_ref[2:3, :]
        h_ref[rows, :] = resid
        centred, scale = centre(resid)
        low = (centred * scale * ln_ref[0:1, :] + ln_ref[1:2, :]).astype(BF)
        a_ref[rows, :] = low
        grad = gy_ref[rows, :]
        out = None
        back = None
        for k in range(2):
            cols = slice(k * chunk, (k + 1) * chunk)
            dcols = slice(hidden + k * chunk, hidden + (k + 1) * chunk)
            pre = nn(low, w_ref[:, cols]) + hb_ref[:, cols]
            square = pre * pre
            inner = math.sqrt(2 / math.pi) * pre * (1.0 + 0.044715 * square)
            tanh = jnp.tanh(inner)
            act = (0.5 * pre * (1.0 + tanh)).astype(BF)
            slope = 0.5 * (1.0 + tanh) + (0.5 * math.sqrt(2 / math.pi)) * pre * (1.0 - tanh * tanh) * (
                1.0 + (3 * 0.044715) * square
            )
            act_ref[rows, cols] = act
            gpre = nn(grad, w_ref[:, dcols]) * slope
            gb_ref[:, cols] = gb_ref[:, cols] + jnp.sum(gpre, axis=0, keepdims=True)
            glow = gpre.astype(BF)
            gp_ref[rows, cols] = glow
            term = nt(act, w_ref[:, dcols])
            out = term if out is None else out + term
            term = nt(glow, w_ref[:, cols])
            back = term if back is None else back + term
        m_ref[rows, :] = out.astype(BF)
        gn_ref[rows, :] = back.astype(BF)
        return carry

    lax.fori_loop(0, blocks, block, 0)
    long_tn(a_ref, gp_ref, full_ref)
    split_rows(order, full_ref, slice(0, hidden), send_ref, keep_ref)
    long_tn(gy_ref, act_ref, full_ref)
    split_rows(order, full_ref, slice(hidden, 2 * hidden), send_ref, keep_ref)


def attention_backward_kernel(bounds, own_ref, got_ref, h_ref, gy_ref, ln_ref, w_ref,
                              qa_ref, ka_ref, va_ref, ob_ref,
                              gh_ref, low_ref, vec_ref, gr_ref, ga_ref, gq_ref, gk_ref, gv_ref):
    half = w_ref.shape[1] // 4
    pairs = half // 128
    blocks = h_ref.shape[0] // QB
    for ref in (vec_ref, gk_ref, gv_ref, gq_ref):
        ref[...] = jnp.zeros_like(ref)

    def second_norm(i, carry):
        rows = rows_at(i)
        grad = own_ref[rows, :].astype(F32) + got_ref[rows, :].astype(F32)
        centred, scale = centre(h_ref[rows, :])
        normal = centred * scale
        gain = grad * ln_ref[0:1, :]
        inner = gain - jnp.mean(gain, axis=-1, keepdims=True)
        inner = inner - normal * jnp.mean(gain * normal, axis=-1, keepdims=True)
        grad_y = gy_ref[rows, :].astype(F32)
        total = grad_y + scale * inner
        gh_ref[rows, :] = total
        for k, item in enumerate((grad * normal, grad, total, grad_y)):
            vec_ref[k : k + 1, :] = vec_ref[k : k + 1, :] + jnp.sum(item, axis=0, keepdims=True)
        low = total.astype(BF)
        low_ref[rows, :] = low
        lane = lax.broadcasted_iota(jnp.int32, (QB, 128), 1)
        local = lane % DH
        cross = head_blocks(1.0, swapped=True)
        for p in range(pairs):
            cols = slice(128 * p, 128 * (p + 1))
            mixed = nn(low, w_ref[:, 3 * half + 128 * p : 3 * half + 128 * (p + 1)]).astype(BF).astype(F32)
            dot = spread(mixed * ob_ref[rows, cols].astype(F32), cross)
            extra = jnp.where(local < 3, three_parts(-dot, local, 0), 0.0)
            ga_ref[rows, 256 * p : 256 * p + 128] = jnp.where(lane < DH, mixed, extra).astype(BF)
            ga_ref[rows, 256 * p + 128 : 256 * p + 256] = jnp.where(lane < DH, extra, mixed).astype(BF)
        return carry

    lax.fori_loop(0, blocks, second_norm, 0)

    def attend(i, carry):
        rows = rows_at(i)

        def keys(j, carry):
            krows = rows_at(j)
            for h in range(2 * pairs):
                cols = slice(128 * h, 128 * (h + 1))
                query, key, out = qa_ref[rows, cols], ka_ref[krows, cols], ga_ref[rows, cols]
                prob = jnp.exp(nt(key, query))
                score = (prob * nt(va_ref[krows, cols], out)).astype(BF)
                gv_ref[krows, cols] = gv_ref[krows, cols] + nn(prob.astype(BF), out)
                gk_ref[krows, cols] = gk_ref[krows, cols] + nn(score, query)
                gq_ref[rows, cols] = gq_ref[rows, cols] + tn(score, key)
            return carry

        return lax.fori_loop(bounds[0, i], bounds[1, i], keys, carry)

    lax.fori_loop(0, blocks, attend, 0)

    def gather(i, carry):
        rows = rows_at(i)
        lane = lax.broadcasted_iota(jnp.int32, (QB, 128), 1)
        for t in range(3 * pairs):
            p = t % pairs
            src = (gq_ref, gk_ref, gv_ref)[t // pairs]
            grad = jnp.where(
                lane < DH, src[rows, 256 * p : 256 * p + 128], src[rows, 256 * p + 128 : 256 * p + 256]
            )
            gr_ref[rows, 128 * t : 128 * (t + 1)] = grad.astype(BF)
        return carry

    lax.fori_loop(0, blocks, gather, 0)


def projection_backward_kernel(order, g_ref, low_ref, ob_ref, w_ref, hd_ref, a_ref, xh_ref, rs_ref,
                               gn_ref, gqb_ref, hv_ref, send_ref, keep_ref, gr_ref, full_ref):
    half = w_ref.shape[1] // 4
    pairs = half // 128
    blocks = g_ref.shape[0] // QB
    for ref in (gqb_ref, hv_ref):
        ref[...] = jnp.zeros_like(ref)

    def head_norm(i, carry):
        rows = rows_at(i)
        mean_blocks = head_blocks(1.0 / DH)
        for t in range(3 * pairs):
            cols = slice(128 * t, 128 * (t + 1))
            grad = g_ref[rows, cols].astype(F32)
            if t < 2 * pairs:
                normal = xh_ref[rows, cols].astype(F32)
                hv_ref[0:1, cols] = hv_ref[0:1, cols] + jnp.sum(grad * normal, axis=0, keepdims=True)
                hv_ref[1:2, cols] = hv_ref[1:2, cols] + jnp.sum(grad, axis=0, keepdims=True)
                gain = grad * hd_ref[0:1, cols]
                inner = gain - spread(gain, mean_blocks) - normal * spread(gain * normal, mean_blocks)
                grad = inner * rs_ref[rows, cols].astype(F32)
            gqb_ref[:, cols] = gqb_ref[:, cols] + jnp.sum(grad, axis=0, keepdims=True)
            gr_ref[rows, cols] = grad.astype(BF)
        gn_ref[rows, :] = nt(gr_ref[rows, :], w_ref[:, : 3 * half]).astype(BF)
        return carry

    lax.fori_loop(0, blocks, head_norm, 0)
    long_tn(a_ref, gr_ref, full_ref.at[:, : 3 * half])
    long_tn(low_ref, ob_ref, full_ref.at[:, 3 * half :])
    split_rows(order, full_ref, slice(0, 4 * half), send_ref, keep_ref)


def call_kernel(kernel, name, scalars, arrays, outs, scratch, flops):
    vmem = pl.BlockSpec(memory_space=pltpu.VMEM)
    smem = pl.BlockSpec(memory_space=pltpu.SMEM)
    size = sum(a.size * a.dtype.itemsize for a in arrays)
    held = size + sum(math.prod(shape) * jnp.dtype(dtype).itemsize for shape, dtype in outs + scratch)
    return pl.pallas_call(
        kernel,
        out_shape=[jax.ShapeDtypeStruct(shape, dtype) for shape, dtype in outs],
        in_specs=[smem] * len(scalars) + [vmem] * len(arrays),
        out_specs=[vmem] * len(outs),
        scratch_shapes=[pltpu.VMEM(shape, dtype) for shape, dtype in scratch],
        compiler_params=pltpu.CompilerParams(vmem_limit_bytes=min(62, held * 5 // 4 // 2**20 + 5) * 2**20),
        cost_estimate=pl.CostEstimate(flops=flops, bytes_accessed=2 * size, transcendentals=0),
        name=name,
    )(*scalars, *arrays)


def body(
    tokens,
    cotangent,
    image_ids,
    step_rates,
    w_qkv,
    w_out,
    w_up,
    w_down,
    norm_gains,
    row_biases,
    head_gains,
    query_bias,
    qkv_bias,
    hidden_bias,
    mom_qkv,
    mom_out,
    mom_up,
    mom_down,
    mom_gains,
    mom_biases,
    mom_head_gains,
    mom_query_bias,
    mom_qkv_bias,
    mom_hidden_bias,
):
    dp_count = lax.axis_size("dp")
    seq_count, length, model_width = tokens.shape
    row_count = seq_count * length
    shard_rows = w_qkv.shape[0]
    half_width = w_qkv.shape[2]
    hidden_part = w_up.shape[1]
    heads_part = half_width // DH
    widths = [3 * half_width, half_width, hidden_part, hidden_part]
    starts = [0, widths[0], widths[0] + widths[1], widths[0] + widths[1] + widths[2]]
    low_weights = jnp.concatenate(
        [w_qkv.reshape(shard_rows, 3 * half_width), w_out.T, w_up, w_down.T], axis=1
    ).astype(BF)
    first_weights = gather_rows(low_weights[:, : starts[2]])
    last_weights = lax.all_gather(low_weights[:, starts[2] :], "dp", axis=0, tiled=True)
    x_low = tokens.reshape(row_count, model_width)
    grad_low = cotangent.reshape(row_count, model_width)
    ids = image_ids.reshape(row_count)
    less = jnp.sum(ids[None, :] < jnp.arange(5)[:, None], axis=1)
    heads_of = ids[::QB]
    tails_of = ids[QB - 1 :: QB]
    bounds = jnp.stack([less[heads_of] // QB, (less[tails_of + 1] + QB - 1) // QB]).astype(jnp.int32)
    local = jnp.arange(128)[None, :] % DH
    hot = jnp.where(ids[:, None] == local, 16.0, 0.0)
    for_query = jnp.where(local == 4, -16.0, hot).astype(BF)
    for_key = jnp.where(local == 4, 16.0, jnp.where((local > 4) & (local < 8), -1.0, hot)).astype(BF)
    scale = DH**-0.5
    pad = jnp.zeros((half_width,), F32)
    head_rows = jnp.stack(
        [
            jnp.concatenate([jnp.tile(head_gains[0] * scale, heads_part), jnp.tile(head_gains[1], heads_part)]),
            jnp.concatenate([jnp.tile(query_bias * scale, heads_part), pad]),
        ]
    )
    order = scatter_order()
    wide = (row_count, 2 * half_width)
    full = (row_count, model_width)
    normed_one, qa, ka, va, mixed, normal, rscale, attn_part = call_kernel(
        forward_kernel,
        "attention_forward",
        [bounds],
        [
            x_low,
            first_weights,
            jnp.stack([norm_gains[0], row_biases[0]]),
            qkv_bias.reshape(1, 3 * half_width),
            head_rows,
            for_query,
            for_key,
        ],
        [(full, BF), (wide, BF), (wide, BF), (wide, BF), ((row_count, half_width), BF), (wide, BF), (wide, BF), (full, BF)],
        [((QB, 2 * half_width), F32)],
        5 * 10**9,
    )
    attn_got = swap_cores(attn_part)
    residual, mlp_part, part_two, hidden_grad, late_send, late_keep = call_kernel(
        mlp_kernel,
        "mlp",
        [order],
        [
            x_low,
            attn_part,
            attn_got,
            last_weights,
            hidden_bias.reshape(1, hidden_part),
            jnp.stack([norm_gains[1], row_biases[2], row_biases[1]]),
            grad_low,
        ],
        [
            (full, F32),
            (full, BF),
            (full, BF),
            ((1, hidden_part), F32),
            ((8, model_width // 16, 2 * hidden_part), BF),
            ((8, model_width // 16, 2 * hidden_part), F32),
        ],
        [
            (full, BF),
            ((row_count, hidden_part), BF),
            ((row_count, hidden_part), BF),
            ((model_width, hidden_part), F32),
        ],
        15 * 10**9,
    )
    fast = dp_count == 16
    two_got = swap_cores(part_two)
    late_got = exchange(late_send, 2, 1) if fast else None
    grad_resid, resid_low, vectors, heads_grad = call_kernel(
        attention_backward_kernel,
        "attention_backward",
        [bounds],
        [part_two, two_got, residual, grad_low, norm_gains[1:2], first_weights, qa, ka, va, mixed],
        [(full, F32), (full, BF), ((4, model_width), F32), ((row_count, 3 * half_width), BF)],
        [(wide, BF), (wide, F32), (wide, F32), (wide, F32)],
        14 * 10**9,
    )
    if fast:
        late_send, late_keep = second_parts(late_keep, after(late_got, heads_grad))
        order = after(order, late_send)
        late_got = exchange(late_send, 1, 2)
    part_one, grad_qkv_bias_local, head_sums, early_send, early_keep = call_kernel(
        projection_backward_kernel,
        "projection_backward",
        [order],
        [heads_grad, resid_low, mixed, first_weights, head_rows, normed_one, normal, rscale],
        [
            (full, BF),
            ((1, 3 * half_width), F32),
            ((2, 2 * half_width), F32),
            ((8, model_width // 16, 4 * half_width), BF),
            ((8, model_width // 16, 4 * half_width), F32),
        ],
        [((row_count, 3 * half_width), BF), ((model_width, 4 * half_width), F32)],
        8 * 10**9,
    )
    old_first = 0.5 * jnp.concatenate([mom_qkv.reshape(shard_rows, 3 * half_width), mom_out.T], axis=1)
    old_last = 0.5 * jnp.concatenate([mom_up, mom_down.T], axis=1)
    one_got = swap_cores(part_one)
    if fast:
        early_got = exchange(early_send, 2, 1)
        parts, late_own = plane_parts(late_keep, late_got)
        late_parts = over_planes(parts)
        early_send, early_keep = second_parts(early_keep, early_got)
        early_got = exchange(early_send, 1, 2)
        parts, early_own = plane_parts(early_keep, early_got)
        early_parts = over_planes(parts)
        late = add_all(late_own, late_parts)
        last_mom = old_last + late
        last_low = last_mom.astype(BF)
        last_planes = [last_low] + over_planes([last_low] * 3)
        early = add_all(early_own, early_parts)
        first_mom = old_first + early
        first_low = first_mom.astype(BF)
        first_planes = [first_low] + over_planes([first_low] * 3)
    else:
        late, early = whole_sum(late_send, late_keep), whole_sum(early_send, early_keep)
        last_mom, first_mom = old_last + late, old_first + early
        last_planes, first_planes = [last_mom.astype(BF)], [first_mom.astype(BF)]
    mlp_out = mlp_part.astype(F32) + swap_cores(mlp_part).astype(F32) + row_biases[3]
    block_out = (residual + mlp_out).reshape(tokens.shape)
    grad_normed_one = part_one.astype(F32) + one_got.astype(F32)
    _, norm_one_pull = jax.vjp(layer_norm, x_low.astype(F32), norm_gains[0], row_biases[0])
    grad_flat_ln, grad_gain_one, grad_shift_one = norm_one_pull(grad_normed_one)
    tokens_grad = (grad_resid + grad_flat_ln).reshape(tokens.shape)
    head_sums = head_sums.reshape(2, 2, heads_part, DH).sum(axis=2)
    grad_head_local = jnp.stack([head_sums[0, 0] * scale, head_sums[0, 1]])
    grad_qshift_local = head_sums[1, 0] * scale
    grad_rows = [early[:, : starts[1]], early[:, starts[1] :], late[:, :hidden_part], late[:, hidden_part:]]
    grad_qkv = grad_rows[0].reshape(shard_rows, 3, half_width)
    grad_out, grad_up, grad_down = grad_rows[1].T, grad_rows[2], grad_rows[3].T
    next_mom_qkv = first_mom[:, : starts[1]].reshape(shard_rows, 3, half_width)
    next_mom_out = first_mom[:, starts[1] :].T
    next_mom_up, next_mom_down = last_mom[:, :hidden_part], last_mom[:, hidden_part:].T
    matrix = own_matrix(first_planes, last_planes, widths)
    own_rows = rows_of_all(orthogonal_rows(matrix, swap_cores(matrix), 4 * shard_rows), shard_rows)
    small = [
        jnp.stack([grad_gain_one, vectors[0]]),
        jnp.stack([grad_shift_one, vectors[2], vectors[1], vectors[3]]),
        grad_qkv_bias_local.reshape(3, half_width),
        hidden_grad.reshape(hidden_part),
        grad_head_local,
        grad_qshift_local,
    ]
    sizes = [part.size for part in small]
    flat = jnp.concatenate([part.reshape(-1) for part in small])
    flat = jnp.pad(flat, (0, -flat.size % 1024)).reshape(-1, 128)
    by_core = sum_everywhere(flat)
    cut = sum(sizes[:4])
    summed = pick(by_core, lax.axis_index("tensor")).reshape(-1)
    heads = (by_core[0] + by_core[1]).reshape(-1)[cut : cut + sizes[4] + sizes[5]]
    pieces = []
    at = 0
    for part, size in zip(small[:4], sizes):
        pieces.append(summed[at : at + size].reshape(part.shape))
        at += size
    grad_gains, grad_biases, grad_qkv_bias, grad_hidden_bias = pieces
    grad_head_gains = heads[: sizes[4]].reshape(grad_head_local.shape)
    grad_query_bias = heads[sizes[4] :]
    rate_muon = step_rates[0]
    new_w_qkv = w_qkv - rate_muon * (0.2 * math.sqrt(max(D, 3 * D))) * own_rows[0][
        :, : 3 * half_width
    ].reshape(shard_rows, 3, half_width)
    new_w_out = w_out - rate_muon * (0.2 * math.sqrt(D)) * own_rows[1][:, 2 * half_width : 3 * half_width].T
    new_w_up = w_up - rate_muon * (0.2 * math.sqrt(max(D, FF))) * own_rows[2][:, :hidden_part]
    new_w_down = w_down - rate_muon * (0.2 * math.sqrt(max(D, FF))) * own_rows[3][:, :hidden_part].T
    rate_vector = step_rates[1] / math.sqrt(row_count * dp_count)
    next_mom_gains = 0.5 * mom_gains + grad_gains
    next_mom_biases = 0.5 * mom_biases + grad_biases
    next_mom_head_gains = 0.5 * mom_head_gains + grad_head_gains
    next_mom_query_bias = 0.5 * mom_query_bias + grad_query_bias
    next_mom_qkv_bias = 0.5 * mom_qkv_bias + grad_qkv_bias
    next_mom_hidden_bias = 0.5 * mom_hidden_bias + grad_hidden_bias
    new_gains = norm_gains - rate_vector * next_mom_gains
    new_biases = row_biases - rate_vector * next_mom_biases
    new_head_gains = head_gains - rate_vector * next_mom_head_gains
    new_query_bias = query_bias - rate_vector * next_mom_query_bias
    new_qkv_bias = qkv_bias - rate_vector * next_mom_qkv_bias
    new_hidden_bias = hidden_bias - rate_vector * next_mom_hidden_bias
    return (
        block_out,
        tokens_grad,
        grad_qkv,
        grad_out,
        grad_up,
        grad_down,
        grad_gains,
        grad_biases,
        grad_head_gains,
        grad_query_bias,
        grad_qkv_bias,
        grad_hidden_bias,
        next_mom_qkv,
        next_mom_out,
        next_mom_up,
        next_mom_down,
        next_mom_gains,
        next_mom_biases,
        next_mom_head_gains,
        next_mom_query_bias,
        next_mom_qkv_bias,
        next_mom_hidden_bias,
        new_w_qkv,
        new_w_out,
        new_w_up,
        new_w_down,
        new_gains,
        new_biases,
        new_head_gains,
        new_query_bias,
        new_qkv_bias,
        new_hidden_bias,
    )


def solution(mesh):
    return jax.shard_map(
        body,
        mesh=mesh,
        in_specs=(
            P("dp", None, None),
            P("dp", None, None),
            P("dp", None),
            P(),
            P("dp", None, "tensor"),
            P("tensor", "dp"),
            P("dp", "tensor"),
            P("tensor", "dp"),
            P(),
            P(),
            P(),
            P(),
            P(None, "tensor"),
            P("tensor"),
            P("dp", None, "tensor"),
            P("tensor", "dp"),
            P("dp", "tensor"),
            P("tensor", "dp"),
            P(),
            P(),
            P(),
            P(),
            P(None, "tensor"),
            P("tensor"),
        ),
        out_specs=(
            P("dp", None, None),
            P("dp", None, None),
            P("dp", None, "tensor"),
            P("tensor", "dp"),
            P("dp", "tensor"),
            P("tensor", "dp"),
            P(),
            P(),
            P(),
            P(),
            P(None, "tensor"),
            P("tensor"),
            P("dp", None, "tensor"),
            P("tensor", "dp"),
            P("dp", "tensor"),
            P("tensor", "dp"),
            P(),
            P(),
            P(),
            P(),
            P(None, "tensor"),
            P("tensor"),
            P("dp", None, "tensor"),
            P("tensor", "dp"),
            P("dp", "tensor"),
            P("tensor", "dp"),
            P(),
            P(),
            P(),
            P(),
            P(None, "tensor"),
            P("tensor"),
        ),
        check_vma=False,
    )
```
